1024 devices in a mesh: seq: 32 (over z_hi, x, y), ch: 32 (over z_lo, core).
Axes of the slice: x: 4, y: 4, z: 32 (z_hi: 2, z_lo: 16; z = z_hi * 16 + z_lo), core: 2. Of those that a mesh axis runs over, the one named last changes fastest.
Arguments:
- query: bfloat16 [4096, 8192], P('seq', 'ch'), may hold values from -6 to 6
- key_in: bfloat16 [4096, 8192], P('seq', 'ch'), may hold values from -6 to 6
- value: bfloat16 [4096, 8192], P('seq', 'ch'), may hold values from -6 to 6
- out_grad: bfloat16 [4096, 8192], P('seq', 'ch'), may hold values from -6 to 6
- filters: float32 [8192, 4096], P(('ch', 'seq')), may hold values from -6 to 6
Outputs:
- grad_query: bfloat16 [4096, 8192], P('seq', 'ch')
- grad_key: bfloat16 [4096, 8192], P('seq', 'ch')
- grad_value: bfloat16 [4096, 8192], P('seq', 'ch')
- filter_grad: float32 [8192, 4096], P(('ch', 'seq'))
The draws below stay inside these ranges and needn't reach their ends.
All inputs are finite; a program needn't handle non-finite values.
Results may differ from the reference program's by a relative error of at most 0.0057.
Values may be sent and summed in bfloat16 or wider, within the bound.
No kernel may reach another device: no remote copies, remote signals or barrier semaphores. Data moves between devices by JAX's collectives and lax.ppermute only.
A program may use at most 32 MiB of HBM per device.

```python
import math
import jax
import jax.numpy as jnp
from jax import lax

D = 8192
L = 4096


def shard_levels(own_key, dims, pieces, low, top_value):
    gain = 1.0
    for position, parts in pieces:
        steps = jax.random.uniform(jax.random.fold_in(jax.random.fold_in(own_key, 6), position), (parts,), jnp.float32, low / len(pieces), top_value / len(pieces))
        gain = gain * jnp.repeat(jnp.exp(steps), dims[position] // parts).reshape((-1,) + (1,) * (len(dims) - 1 - position))
    return gain


def scatter_about(rng, shape, width, most, split=(), dtype=jnp.bfloat16):
    values = jax.random.normal(rng, shape, jnp.float32) * width
    if len(split) > 0:
        values = shard_levels(rng, shape, split, -0.22, 0.18) * values
    return jnp.clip(values, min=-most, max=most).astype(dtype)


def setup_inputs(seed: int = 0) -> dict:
    seeds = jax.random.split(jax.random.key(seed), 6)
    return {
        "query": scatter_about(seeds[0], (L, D), 1.0, 6.0, ((0, 32), (1, 32))),
        "key_in": scatter_about(seeds[1], (L, D), 1.0, 6.0, ((0, 32), (1, 32))),
        "value": scatter_about(seeds[2], (L, D), 1.0, 6.0, ((0, 32), (1, 32))),
        "out_grad": scatter_about(seeds[3], (L, D), 1.0, 6.0, ((0, 32), (1, 32))),
        "filters": scatter_about(seeds[4], (D, L), 1.0, 6.0, ((0, 1024),), jnp.float32),
    }


def spectra_block(blocks):
    mixed_blk, gated_blk, filter_blk = blocks
    length = mixed_blk.shape[-1]
    padded_len = 2 * length
    factor = 1.0 / math.sqrt(length)
    spec_mixed = jnp.fft.rfft(mixed_blk.astype(jnp.float32), n=padded_len, axis=-1)
    spec_gated = jnp.fft.rfft(gated_blk.astype(jnp.float32), n=padded_len, axis=-1)
    spec_filter = jnp.fft.rfft(filter_blk.astype(jnp.float32), n=padded_len, axis=-1)
    conv_out = jnp.fft.irfft(spec_mixed * spec_filter, n=padded_len, axis=-1)[..., :length] * factor
    input_grad = jnp.fft.irfft(spec_gated * jnp.conj(spec_filter), n=padded_len, axis=-1)[..., :length] * factor
    filter_grad = jnp.fft.irfft(spec_gated * jnp.conj(spec_mixed), n=padded_len, axis=-1)[..., :length] * factor
    return (conv_out.astype(jnp.bfloat16), input_grad.astype(jnp.bfloat16), filter_grad.astype(jnp.float32))

def reference(query, key_in, value, out_grad, filters):
    seq_len, channels = query.shape
    block_size = min(256, channels)
    mixed = (key_in.astype(jnp.float32) * value.astype(jnp.float32)).astype(jnp.bfloat16)
    gated = (out_grad.astype(jnp.float32) * query.astype(jnp.float32)).astype(jnp.bfloat16)

    def blocked(array):
        return array.T.reshape(channels // block_size, block_size, seq_len)
    conv_out, input_grad, filter_grad = lax.map(spectra_block, (blocked(mixed), blocked(gated), filters.reshape(channels // block_size, block_size, seq_len)))
    conv_out = conv_out.reshape(channels, seq_len).T
    input_grad = input_grad.reshape(channels, seq_len).T
    grad_query = (out_grad.astype(jnp.float32) * conv_out.astype(jnp.float32)).astype(jnp.bfloat16)
    grad_key = (input_grad.astype(jnp.float32) * value.astype(jnp.float32)).astype(jnp.bfloat16)
    grad_value = (input_grad.astype(jnp.float32) * key_in.astype(jnp.float32)).astype(jnp.bfloat16)
    return (grad_query, grad_key, grad_value, filter_grad.reshape(channels, seq_len))
```

```python
import math

import jax
import jax.numpy as jnp
import numpy as np
from jax import lax
from jax.experimental import pallas as pl
from jax.experimental.pallas import tpu as pltpu
from jax.sharding import Mesh
from jax.sharding import PartitionSpec as P

BLK, CH, LANE = 16, 8, 128
ROWS = BLK * CH
HALF = BLK * LANE
f32, bf16 = jnp.float32, jnp.bfloat16


def split_terms(values):
    high = values.astype(np.float32).astype(bf16)
    low = (values - high.astype(np.float64)).astype(np.float32).astype(bf16)
    return high, low


def tables():
    odd = np.arange(BLK) + 0.5
    outer = 2 * np.pi * np.outer(odd, np.arange(BLK)) / (2 * BLK)
    eye = np.eye(CH)
    first = np.concatenate([np.kron(np.cos(outer), eye), np.kron(-np.sin(outer), eye)], 0)
    scale = 2.0 / (2 * HALF) / math.sqrt(2 * HALF)
    inner = 2 * np.pi * np.outer(np.arange(LANE), np.arange(LANE)) / LANE
    cosine, sine = np.cos(inner), np.sin(inner)
    wide = np.block([[cosine, -sine], [sine, cosine]])
    turn = 2 * np.pi * np.outer(odd, np.arange(LANE)) / (2 * HALF)
    turn = np.repeat(turn[:, None], CH, 1).reshape(ROWS, LANE)
    twiddle = np.stack([np.cos(turn), np.sin(turn)]).astype(np.float32)
    first_both = np.concatenate(split_terms(first), 1)
    wide_both = np.stack(split_terms(wide))
    back_both = np.stack(split_terms(wide.T))
    last_both = np.stack(split_terms(first.T * scale))
    return first_both, wide_both, back_both, last_both, twiddle


def dot(left, right):
    return jnp.dot(left, right, preferred_element_type=f32)


def terms(values):
    high = values.astype(bf16)
    return high, (values - high.astype(f32)).astype(bf16)


def spectra(signals, first, wide, twiddle):
    both = jnp.concatenate(signals, 1)
    part = dot(first[...], jnp.concatenate([both, both], 0))
    cosine, sine = twiddle[0], twiddle[1]
    turned = []
    for at in range(len(signals)):
        cols = slice(at * LANE, (at + 1) * LANE)
        real, imag = part[:ROWS, cols], part[ROWS:, cols]
        turned.append(
            jnp.concatenate([real * cosine + imag * sine, imag * cosine - real * sine], 1)
        )
    high, low = terms(jnp.concatenate(turned, 0))
    out = dot(high, wide[0]) + dot(low, wide[0]) + dot(high, wide[1])
    return [out[at * ROWS : (at + 1) * ROWS] for at in range(len(signals))]


def signals_of(spectrum_list, back, last, twiddle):
    high, low = terms(jnp.concatenate(spectrum_list, 0))
    inner = dot(high, back[0]) + dot(low, back[0]) + dot(high, back[1])
    cosine, sine = twiddle[0], twiddle[1]
    turned = []
    for at in range(len(spectrum_list)):
        rows = slice(at * ROWS, (at + 1) * ROWS)
        real, imag = inner[rows, :LANE], inner[rows, LANE:]
        turned.append(
            jnp.concatenate([real * cosine - imag * sine, real * sine + imag * cosine], 0)
        )
    high, low = terms(jnp.concatenate(turned, 1))
    out = dot(last[0], high) + dot(last[0], low) + dot(last[1], high)
    return [out[:, at * LANE : (at + 1) * LANE] for at in range(len(spectrum_list))]


def times(left, right):
    a, b, c, d = left[:, :LANE], left[:, LANE:], right[:, :LANE], right[:, LANE:]
    return jnp.concatenate([a * c - b * d, a * d + b * c], 1)


def times_conj(left, right, sign=1.0):
    a, b, c, d = left[:, :LANE], left[:, LANE:], right[:, :LANE], sign * right[:, LANE:]
    return jnp.concatenate([a * c + b * d, b * c - a * d], 1)


def alternate():
    k1 = lax.broadcasted_iota(jnp.int32, (ROWS, LANE), 0) // CH
    return (1 - 2 * (k1 % 2)).astype(f32)


def shifted(values, way):
    signs = way * alternate()
    return jnp.concatenate([signs * values[:, LANE:], -signs * values[:, :LANE]], 1)


def unpaired(pair):
    wide = pair.astype(f32)
    return (
        wide[:, :CH].reshape(ROWS, LANE),
        wide[:, CH:].reshape(ROWS, LANE),
    )


def paired(one, two):
    wide = jnp.concatenate([one.reshape(BLK, CH, LANE), two.reshape(BLK, CH, LANE)], 1)
    return wide.astype(bf16)


def gates_body(query, key_in, value, out_grad, sent):
    mixed = (key_in[...].astype(f32) * value[...].astype(f32)).astype(bf16).astype(f32)
    gated = (out_grad[...].astype(f32) * query[...].astype(f32)).astype(bf16).astype(f32)
    mixed = mixed.T.reshape(2, BLK, CH, LANE)
    gated = gated.T.reshape(2, BLK, CH, LANE)
    for half in range(2):
        sent[:, half] = jnp.concatenate([mixed[half], gated[half]], 1).astype(bf16)


def near_body(half, came, filters, first, wide, back, last, twiddle, own_spec, filt_spec, sent):
    side = half[0]
    flag = side.astype(f32)
    mix, gate = unpaired(came[:, side])
    filt = [filters[:, at * LANE : (at + 1) * LANE] for at in range(2 * BLK)]
    filt_lo = jnp.concatenate(filt[:BLK], 0)
    filt_hi = jnp.concatenate(filt[BLK:], 0)
    spec_mix, spec_gate, spec_lo, spec_hi = spectra(
        [mix.astype(bf16), gate.astype(bf16), filt_lo.astype(bf16), filt_hi.astype(bf16)],
        first,
        wide,
        twiddle,
    )
    cross = spec_hi + shifted(spec_lo, -1.0)
    chosen = spec_mix + flag * (spec_gate - spec_mix)
    far = signals_of(
        [times_conj(chosen, cross, 2.0 * flag - 1.0)], back, last, twiddle
    )[0]
    own_spec[0] = spec_mix
    own_spec[1] = spec_gate
    filt_spec[0] = spec_lo
    filt_spec[1] = cross
    sent[0] = came[:, 1 - side]
    sent[1] = paired(filt_lo, far)


def away_body(half, came, first, wide, twiddle, away_spec):
    mix, gate = unpaired(came[:, 1 - half[0]])
    spec_mix, spec_gate = spectra([mix.astype(bf16), gate.astype(bf16)], first, wide, twiddle)
    away_spec[0] = spec_mix
    away_spec[1] = spec_gate


def far_body(
    half, came, own_spec, filt_spec, away_spec, first, wide, back, last, twiddle, sent, filter_grad
):
    side = half[0]
    flag = side.astype(f32)
    mix, gate = unpaired(came[0])
    away_lo, away_far = unpaired(came[1])
    other_mix, other_gate, spec_away = spectra(
        [mix.astype(bf16), gate.astype(bf16), away_lo.astype(bf16)], first, wide, twiddle
    )
    own_mix, own_gate = own_spec[0], own_spec[1]
    spec_lo, cross = filt_spec[0], filt_spec[1]
    early_mix = own_mix + flag * (other_mix - own_mix)
    late_gate = other_gate + flag * (own_gate - other_gate)
    lag_cross = times_conj(late_gate, early_mix)
    lag_same = times_conj(own_gate, own_mix) + times_conj(other_gate, other_mix)
    chosen = other_gate + flag * (other_mix - other_gate)
    extra = times_conj(chosen, cross, 1.0 - 2.0 * flag)
    conv = times(own_mix, spec_lo) + flag * extra
    grad = times_conj(own_gate, spec_lo) + (1.0 - flag) * extra
    conv_away = times(away_spec[0], spec_away)
    grad_away = times_conj(away_spec[1], spec_away)
    conv, grad, conv_away, grad_away, lag_lo, lag_hi = signals_of(
        [conv, grad, conv_away, grad_away, lag_same + shifted(lag_cross, 1.0), lag_cross],
        back,
        last,
        twiddle,
    )
    sent[:, side] = paired(conv, grad)
    sent[:, 1 - side] = paired(
        conv_away + flag * away_far, grad_away + (1.0 - flag) * away_far
    )
    for at in range(BLK):
        rows = slice(at * CH, (at + 1) * CH)
        filter_grad[:, at * LANE : (at + 1) * LANE] = lag_lo[rows]
        filter_grad[:, HALF + at * LANE : HALF + (at + 1) * LANE] = lag_hi[rows]


def last_body(came, key_in, value, out_grad, grad_query, grad_key, grad_value):
    wide = came[...].astype(f32)
    conv = wide[:, :, :CH].transpose(1, 0, 2, 3).reshape(2 * ROWS, LANE).T
    grad = wide[:, :, CH:].transpose(1, 0, 2, 3).reshape(2 * ROWS, LANE).T
    grad_query[...] = (out_grad[...].astype(f32) * conv).astype(bf16)
    grad_key[...] = (grad * value[...].astype(f32)).astype(bf16)
    grad_value[...] = (grad * key_in[...].astype(f32)).astype(bf16)


def call(body, outs, *operands, scalar=False, name):
    specs = [pl.BlockSpec(memory_space=pltpu.VMEM) for _ in operands]
    if scalar:
        specs[0] = pl.BlockSpec(memory_space=pltpu.SMEM)
    return pl.pallas_call(
        body,
        out_shape=[jax.ShapeDtypeStruct(*out) for out in outs],
        in_specs=specs,
        out_specs=[pl.BlockSpec(memory_space=pltpu.VMEM) for _ in outs],
        name=name,
    )(*operands)


PAIR = ((BLK, 2, 2 * CH, LANE), bf16)


def swap_pieces(pieces):
    return lax.all_to_all(
        pieces.reshape(BLK, 4 * CH, LANE), ("x", "y"), split_axis=0, concat_axis=0, tiled=True
    ).reshape(PAIR[0])


def on_device(query, key_in, value, out_grad, filters):
    half = lax.axis_index("z_hi").reshape(1).astype(jnp.int32)
    first, wide, back, last, twiddle = (jnp.asarray(table) for table in tables())
    (sent,) = call(gates_body, [PAIR], query, key_in, value, out_grad, name="gates")
    came = swap_pieces(sent)
    spec = ((2, ROWS, 2 * LANE), f32)
    own_spec, filt_spec, sent = call(
        near_body,
        [spec, spec, ((2, BLK, 2 * CH, LANE), bf16)],
        half, came, filters, first, wide, back, last, twiddle,
        scalar=True, name="near",
    )
    crossed = lax.ppermute(sent, "z_hi", [(0, 1), (1, 0)])
    (away_spec,) = call(
        away_body, [spec], half, came, first, wide, twiddle, scalar=True, name="away"
    )
    sent, filter_grad = call(
        far_body,
        [PAIR, (filters.shape, f32)],
        half, crossed, own_spec, filt_spec, away_spec, first, wide, back, last, twiddle,
        scalar=True, name="far",
    )
    came = swap_pieces(sent)
    gate = (query.shape, bf16)
    grads = call(
        last_body, [gate] * 3, came, key_in, value, out_grad, name="last"
    )
    return (*grads, filter_grad)


def solution(mesh):
    axes = (2, 4, 4, 16, 2)
    fine = Mesh(mesh.devices.reshape(axes), ("z_hi", "x", "y", "z_lo", "core"))
    seq, ch = ("z_hi", "x", "y"), ("z_lo", "core")
    gate, filt = P(seq, ch), P(ch + seq, None)
    return jax.shard_map(
        on_device,
        mesh=fine,
        in_specs=(gate, gate, gate, gate, filt),
        out_specs=(gate, gate, gate, filt),
        check_vma=False,
    )
```

```python
import math

import jax
import jax.numpy as jnp
import numpy as np
from jax import lax
from jax.experimental import pallas as pl
from jax.experimental.pallas import tpu as pltpu
from jax.sharding import Mesh
from jax.sharding import PartitionSpec as P

BLK, CH, LANE = 16, 8, 128
ROWS = BLK * CH
HALF = BLK * LANE
f32, bf16 = jnp.float32, jnp.bfloat16


def split_terms(values):
    high = values.astype(np.float32).astype(bf16)
    low = (values - high.astype(np.float64)).astype(np.float32).astype(bf16)
    return high, low


def tables():
    odd = np.arange(BLK) + 0.5
    outer = 2 * np.pi * np.outer(odd, np.arange(BLK)) / (2 * BLK)
    eye = np.eye(CH)
    first = np.concatenate([np.kron(np.cos(outer), eye), np.kron(-np.sin(outer), eye)], 0)
    scale = 2.0 / (2 * HALF) / math.sqrt(2 * HALF)
    inner = 2 * np.pi * np.outer(np.arange(LANE), np.arange(LANE)) / LANE
    cosine, sine = np.cos(inner), np.sin(inner)
    wide = np.block([[cosine, -sine], [sine, cosine]])
    turn = 2 * np.pi * np.outer(odd, np.arange(LANE)) / (2 * HALF)
    turn = np.repeat(turn[:, None], CH, 1).reshape(ROWS, LANE)
    twiddle = np.stack([np.cos(turn), np.sin(turn)]).astype(np.float32)
    first_both = np.concatenate(split_terms(first), 1)
    wide_both = np.stack(split_terms(wide))
    last_both = np.stack(split_terms(first.T * scale))
    return first_both, wide_both, last_both, twiddle


def dot(left, right):
    return jnp.dot(left, right, preferred_element_type=f32)


def dot_back(left, right):
    return lax.dot_general(left, right, (((1,), (1,)), ((), ())), preferred_element_type=f32)


def terms(values):
    high = values.astype(bf16)
    return high, (values - high.astype(f32)).astype(bf16)


def spectra(signals, first, wide, twiddle):
    both = jnp.concatenate(signals, 1)
    part = dot(first[...], jnp.concatenate([both, both], 0))
    cosine, sine = twiddle[0], twiddle[1]
    turned = []
    for at in range(len(signals)):
        cols = slice(at * LANE, (at + 1) * LANE)
        real, imag = part[:ROWS, cols], part[ROWS:, cols]
        turned.append(
            jnp.concatenate([real * cosine + imag * sine, imag * cosine - real * sine], 1)
        )
    high, low = terms(jnp.concatenate(turned, 0))
    out = dot(high, wide[0]) + dot(low, wide[0]) + dot(high, wide[1])
    return [out[at * ROWS : (at + 1) * ROWS] for at in range(len(signals))]


def signals_of(spectrum_list, wide, last, twiddle):
    high, low = terms(jnp.concatenate(spectrum_list, 0))
    inner = dot_back(high, wide[0]) + dot_back(low, wide[0]) + dot_back(high, wide[1])
    cosine, sine = twiddle[0], twiddle[1]
    turned = []
    for at in range(len(spectrum_list)):
        rows = slice(at * ROWS, (at + 1) * ROWS)
        real, imag = inner[rows, :LANE], inner[rows, LANE:]
        turned.append(
            jnp.concatenate([real * cosine - imag * sine, real * sine + imag * cosine], 0)
        )
    high, low = terms(jnp.concatenate(turned, 1))
    out = dot(last[0], high) + dot(last[0], low) + dot(last[1], high)
    return [out[:, at * LANE : (at + 1) * LANE] for at in range(len(spectrum_list))]


def times(left, right):
    a, b, c, d = left[:, :LANE], left[:, LANE:], right[:, :LANE], right[:, LANE:]
    return jnp.concatenate([a * c - b * d, a * d + b * c], 1)


def times_conj(left, right, sign=1.0):
    a, b, c, d = left[:, :LANE], left[:, LANE:], right[:, :LANE], sign * right[:, LANE:]
    return jnp.concatenate([a * c + b * d, b * c - a * d], 1)


def alternate():
    k1 = lax.broadcasted_iota(jnp.int32, (ROWS, LANE), 0) // CH
    return (1 - 2 * (k1 % 2)).astype(f32)


def shifted(values, way):
    signs = way * alternate()
    return jnp.concatenate([signs * values[:, LANE:], -signs * values[:, :LANE]], 1)


def unpaired(pair):
    wide = pair.astype(f32)
    return (
        wide[:, :CH].reshape(ROWS, LANE),
        wide[:, CH:].reshape(ROWS, LANE),
    )


def paired(one, two):
    wide = jnp.concatenate([one.reshape(BLK, CH, LANE), two.reshape(BLK, CH, LANE)], 1)
    return wide.astype(bf16)


def gates_body(query, key_in, value, out_grad, filters, sent, filt_pair):
    mixed = (key_in[...].astype(f32) * value[...].astype(f32)).astype(bf16).astype(f32)
    gated = (out_grad[...].astype(f32) * query[...].astype(f32)).astype(bf16).astype(f32)
    mixed = mixed.T.reshape(2, BLK, CH, LANE)
    gated = gated.T.reshape(2, BLK, CH, LANE)
    for half in range(2):
        sent[:, half] = jnp.concatenate([mixed[half], gated[half]], 1).astype(bf16)
    filt = [filters[:, at * LANE : (at + 1) * LANE] for at in range(2 * BLK)]
    filt_pair[...] = paired(jnp.concatenate(filt[:BLK], 0), jnp.concatenate(filt[BLK:], 0))


def near_body(half, came, filt_pair, first, wide, last, twiddle, own_spec, filt_spec, sent):
    side = half[0]
    flag = side.astype(f32)
    mix, gate = unpaired(came[:, side])
    filt_lo, filt_hi = unpaired(filt_pair[...])
    spec_mix, spec_gate, spec_lo, spec_hi = spectra(
        [mix.astype(bf16), gate.astype(bf16), filt_lo.astype(bf16), filt_hi.astype(bf16)],
        first,
        wide,
        twiddle,
    )
    cross = spec_hi + shifted(spec_lo, -1.0)
    chosen = spec_mix + flag * (spec_gate - spec_mix)
    far = signals_of(
        [times_conj(chosen, cross, 2.0 * flag - 1.0)], wide, last, twiddle
    )[0]
    own_spec[0] = spec_mix
    own_spec[1] = spec_gate
    filt_spec[0] = spec_lo
    filt_spec[1] = cross
    sent[0] = came[:, 1 - side]
    sent[1] = paired(filt_lo, far)


def away_body(half, came, first, wide, twiddle, away_spec):
    mix, gate = unpaired(came[:, 1 - half[0]])
    spec_mix, spec_gate = spectra([mix.astype(bf16), gate.astype(bf16)], first, wide, twiddle)
    away_spec[0] = spec_mix
    away_spec[1] = spec_gate


def far_body(
    half, came, own_spec, filt_spec, away_spec, first, wide, last, twiddle, sent, filter_grad
):
    side = half[0]
    flag = side.astype(f32)
    mix, gate = unpaired(came[0])
    away_lo, away_far = unpaired(came[1])
    other_mix, other_gate, spec_away = spectra(
        [mix.astype(bf16), gate.astype(bf16), away_lo.astype(bf16)], first, wide, twiddle
    )
    own_mix, own_gate = own_spec[0], own_spec[1]
    spec_lo, cross = filt_spec[0], filt_spec[1]
    early_mix = own_mix + flag * (other_mix - own_mix)
    late_gate = other_gate + flag * (own_gate - other_gate)
    lag_cross = times_conj(late_gate, early_mix)
    lag_same = times_conj(own_gate, own_mix) + times_conj(other_gate, other_mix)
    chosen = other_gate + flag * (other_mix - other_gate)
    extra = times_conj(chosen, cross, 1.0 - 2.0 * flag)
    conv = times(own_mix, spec_lo) + flag * extra
    grad = times_conj(own_gate, spec_lo) + (1.0 - flag) * extra
    conv_away = times(away_spec[0], spec_away)
    grad_away = times_conj(away_spec[1], spec_away)
    conv, grad, conv_away, grad_away, lag_lo, lag_hi = signals_of(
        [conv, grad, conv_away, grad_away, lag_same + shifted(lag_cross, 1.0), lag_cross],
        wide,
        last,
        twiddle,
    )
    sent[:, side] = paired(conv, grad)
    sent[:, 1 - side] = paired(
        conv_away + flag * away_far, grad_away + (1.0 - flag) * away_far
    )
    for at in range(BLK):
        rows = slice(at * CH, (at + 1) * CH)
        filter_grad[:, at * LANE : (at + 1) * LANE] = lag_lo[rows]
        filter_grad[:, HALF + at * LANE : HALF + (at + 1) * LANE] = lag_hi[rows]


def last_body(came, key_in, value, out_grad, grad_query, grad_key, grad_value):
    wide = came[...].astype(f32)
    conv = wide[:, :, :CH].transpose(1, 0, 2, 3).reshape(2 * ROWS, LANE).T
    grad = wide[:, :, CH:].transpose(1, 0, 2, 3).reshape(2 * ROWS, LANE).T
    grad_query[...] = (out_grad[...].astype(f32) * conv).astype(bf16)
    grad_key[...] = (grad * value[...].astype(f32)).astype(bf16)
    grad_value[...] = (grad * key_in[...].astype(f32)).astype(bf16)


def near_memory(array):
    return pltpu.with_memory_space_constraint(array, pltpu.VMEM)


def call(body, outs, *operands, scalar=False, far_in=False, far_out=False, name):
    specs = [pl.BlockSpec(memory_space=pltpu.VMEM) for _ in operands]
    if scalar:
        specs[0] = pl.BlockSpec(memory_space=pltpu.SMEM)
    if not far_in:
        operands = (*operands[:scalar], *map(near_memory, operands[scalar:]))
    kind = jax.ShapeDtypeStruct if far_out else pltpu.VMEM
    return pl.pallas_call(
        body,
        out_shape=[kind(*out) for out in outs],
        in_specs=specs,
        out_specs=[pl.BlockSpec(memory_space=pltpu.VMEM) for _ in outs],
        name=name,
    )(*operands)


PAIR = ((BLK, 2, 2 * CH, LANE), bf16)
ONE = ((BLK, 2 * CH, LANE), bf16)


def swap_pieces(pieces):
    return lax.all_to_all(
        pieces.reshape(BLK, 4 * CH, LANE), ("x", "y"), split_axis=0, concat_axis=0, tiled=True
    ).reshape(PAIR[0])


def on_device(query, key_in, value, out_grad, filters):
    half = lax.axis_index("z_hi").reshape(1).astype(jnp.int32)
    first, wide, last, twiddle = (jnp.asarray(table) for table in tables())
    sent, filt_pair = call(
        gates_body, [PAIR, ONE], query, key_in, value, out_grad, filters, far_in=True, name="gates"
    )
    came = swap_pieces(sent)
    spec = ((2, ROWS, 2 * LANE), f32)
    own_spec, filt_spec, sent = call(
        near_body,
        [spec, spec, ((2, BLK, 2 * CH, LANE), bf16)],
        half, came, filt_pair, first, wide, last, twiddle,
        scalar=True, name="near",
    )
    crossed = lax.ppermute(sent, "z_hi", [(0, 1), (1, 0)])
    (away_spec,) = call(
        away_body, [spec], half, came, first, wide, twiddle, scalar=True, name="away"
    )
    sent, filter_grad = call(
        far_body,
        [PAIR, (filters.shape, f32)],
        half, crossed, own_spec, filt_spec, away_spec, first, wide, last, twiddle,
        scalar=True, name="far",
    )
    came = swap_pieces(sent)
    gate = (query.shape, bf16)
    grads = call(
        last_body, [gate] * 3, came, key_in, value, out_grad, far_out=True, name="last"
    )
    return (*grads, filter_grad)


def solution(mesh):
    axes = (2, 4, 4, 16, 2)
    fine = Mesh(mesh.devices.reshape(axes), ("z_hi", "x", "y", "z_lo", "core"))
    seq, ch = ("z_hi", "x", "y"), ("z_lo", "core")
    gate, filt = P(seq, ch), P(ch + seq, None)
    return jax.shard_map(
        on_device,
        mesh=fine,
        in_specs=(gate, gate, gate, gate, filt),
        out_specs=(gate, gate, gate, filt),
        check_vma=False,
    )
```
